32 devices in a mesh: group: 4 (over z), tensor: 4 (over y, core), role: 2 (over x).
Axes of the slice: x: 2, y: 2, z: 4, core: 2. Of those that a mesh axis runs over, the one named last changes fastest.
Arguments:
- queries: bfloat16 [4096, 4096], P(('group', 'role'), 'tensor'), may hold values from -8 to 8
- keys_values: bfloat16 [2, 4096, 1024], P(None, ('group', 'role')), may hold values from -8 to 8
- doc_ids: int32 [4096], P(('group', 'role')), may hold values from 0 to 15, never falling along the last dimension, each value on 1 to 1024 neighbouring positions
Outputs:
- attended: bfloat16 [4096, 4096], P(('group', 'role'), 'tensor')
The draws below stay inside these ranges and needn't reach their ends.
All inputs are finite; a program needn't handle non-finite values.
Results may differ from the reference program's by a relative error of at most 0.0036.
Values may be sent and summed in bfloat16 or wider, within the bound.
A program may use at most 64 MiB of HBM per device.

```python
import math
import jax
import jax.numpy as jnp
import numpy as np
from jax import lax

HEADS = 32
KV_HEADS = 8
HD = 128
SEQ = 1024
TOKENS = 4096
DOCS = 16
N_GROUP = 4


def joint_draw(key):
    base = jax.random.fold_in(key, 7301)
    key_query, key_key, key_value = jax.random.split(base, 3)
    query_new = jax.random.truncated_normal(key_query, -4.0, 4.0, (TOKENS, HEADS, HD), jnp.float32)
    key_new = jax.random.truncated_normal(key_key, -4.0, 4.0, (TOKENS, KV_HEADS, HD), jnp.float32)
    value_raw = jax.random.truncated_normal(key_value, -4.0, 4.0, (TOKENS, KV_HEADS, HD), jnp.float32)
    queries = query_new.reshape(TOKENS, HEADS * HD)
    pairs = jnp.stack([key_new, value_raw]).reshape(2, TOKENS, KV_HEADS * HD)
    return (queries, pairs)


def draw_queries(key, part):
    return joint_draw(key)[0].astype(jnp.bfloat16)


def draw_keys_values(key, part):
    return joint_draw(key)[1].astype(jnp.bfloat16)


def split_up(number_of, total, bound, lean):
    weights = [(1 << 20) // math.isqrt(standing ** lean) + 1 for standing in range(2, number_of + 1)]
    surplus, counts = total - bound - (number_of - 1), [1] * (number_of - 1)
    while surplus > 0:
        candidates = [i for i in range(number_of - 1) if counts[i] < bound]
        mass, left = sum([weights[i] for i in candidates]), surplus
        for i in candidates:
            addition = min(bound - counts[i], max(1, left * weights[i] // mass), surplus)
            counts[i] = counts[i] + addition
            surplus = surplus - addition
    return np.array([bound] + counts)


def uneven(stream_key, amount, total, bound, skew):
    if amount == 2:
        one = jax.random.randint(stream_key, (), max(1, total - bound), min(bound, total - 1) + 1)
        return jnp.stack([one, total - one])
    tallies = jnp.asarray(split_up(amount, total, bound, skew), jnp.int32)
    couples = (amount - 1) // 2
    source_of, receiver = tallies[1:1 + 2 * couples:2], tallies[2:2 + 2 * couples:2]
    slack = jnp.minimum(source_of - 1, bound - receiver)
    passed = jax.random.randint(jax.random.fold_in(stream_key, 1), (couples,), 0, 1 << 20) % (slack + 1)
    tallies = tallies.at[1:1 + 2 * couples:2].set(source_of - passed).at[2:2 + 2 * couples:2].set(receiver + passed)
    return tallies[jax.random.permutation(jax.random.fold_in(stream_key, 2), amount)]


def setup_inputs(seed: int = 0) -> dict:
    seeds = jax.random.split(jax.random.key(seed), 4)
    return {
        "queries": draw_queries(jax.random.fold_in(seeds[3], 71), 0),
        "keys_values": draw_keys_values(jax.random.fold_in(seeds[3], 71), 0),
        "doc_ids": jnp.searchsorted(jnp.cumsum(uneven(seeds[2], DOCS, TOKENS, SEQ, 2)), jnp.arange(TOKENS), side="right").astype(jnp.int32),
    }


def reference(queries, keys_values, doc_ids):
    group_width = HEADS // KV_HEADS
    scaling = 1.0 / math.sqrt(HD)
    grouped_q = queries.reshape(N_GROUP, SEQ, KV_HEADS, group_width, HD)
    grouped_kv = keys_values.reshape(2, N_GROUP, SEQ, KV_HEADS, HD)
    grouped_ids = doc_ids.reshape(N_GROUP, SEQ)
    position = jnp.arange(SEQ, dtype=jnp.int32)

    def one_group(inputs):
        query_block, key_block, value_block, id_block = inputs
        visible = (position[None, :] <= position[:, None]) & (id_block[None, :] == id_block[:, None])

        def one_head(head_inputs):
            head_q, head_k, head_v = head_inputs
            scores = jnp.einsum('qgd,kd->gqk', head_q.astype(jnp.float32), head_k.astype(jnp.float32)) * scaling
            scores = jnp.where(visible[None], scores, -1e+30)
            largest = lax.optimization_barrier(jnp.max(scores, axis=-1, keepdims=True))
            weights = jnp.where(visible[None], jnp.exp(scores - largest), 0.0)
            totals = lax.optimization_barrier(jnp.sum(weights, axis=-1))
            rounded = weights.astype(jnp.bfloat16)
            summed = jnp.einsum('gqk,kd->qgd', rounded.astype(jnp.float32), head_v.astype(jnp.float32))
            return (summed / jnp.transpose(totals)[:, :, None]).astype(jnp.bfloat16)
        heads_out = lax.map(one_head, (jnp.moveaxis(query_block, 1, 0), jnp.moveaxis(key_block, 1, 0), jnp.moveaxis(value_block, 1, 0)))
        return jnp.moveaxis(heads_out, 0, 1).reshape(SEQ, HEADS * HD)
    result = lax.map(one_group, (grouped_q, grouped_kv[0], grouped_kv[1], grouped_ids))
    return result.reshape(N_GROUP * SEQ, HEADS * HD)
```

```python
import functools
import math

import jax
import jax.numpy as jnp
from jax import lax
from jax.experimental import pallas as pl
from jax.experimental.pallas import tpu as pltpu
from jax.sharding import PartitionSpec as P

HD = 128
TILE = 128
HIDDEN = -1e30
MESH = pl.DeviceIdType.MESH


def dot_t(a, b):
    return lax.dot_general(a, b, (((1,), (1,)), ((), ())), preferred_element_type=jnp.float32)


def dot(a, b):
    return lax.dot_general(a, b, (((1,), (0,)), ((), ())), preferred_element_type=jnp.float32)


def kernel(
    n, kvc, share, group_width, q_hbm, kv_hbm, ids_ref, out_hbm,
    q, k_own, v_own, k_in, v_in, ids_in, ids_col, bias, weights, acc, top, total, out_buf,
    q_sem, k_sem, v_sem, out_sem, ids_send, ids_recv, k_send, k_recv, v_send, v_recv,
):
    rows = q_hbm.shape[0]
    heads = kvc * share
    tiles = rows // TILE
    width = share * HD
    role = lax.axis_index("role")
    first_kv = lax.axis_index("tensor") * heads // group_width
    rate = math.log2(math.e) / math.sqrt(HD)

    barrier = pltpu.get_barrier_semaphore()
    for k in range(1, n):
        pl.semaphore_signal(
            barrier, inc=1, device_id={"role": lax.rem(role + k, n)}, device_id_type=MESH
        )

    def side(which, c):
        return kv_hbm.at[which, :, pl.ds(pl.multiple_of((first_kv + c) * HD, HD), HD)]

    def q_copy(c):
        cols = slice(c * width, (c + 1) * width)
        return pltpu.make_async_copy(q_hbm.at[:, cols], q.at[:, cols], q_sem.at[c])

    def k_copy(c):
        return pltpu.make_async_copy(side(0, c), k_own.at[c], k_sem.at[c])

    def v_copy(c):
        return pltpu.make_async_copy(side(1, c), v_own.at[c], v_sem.at[c])

    def out_copy(c):
        cols = slice(c * width, (c + 1) * width)
        return pltpu.make_async_copy(out_buf.at[:, cols], out_hbm.at[:, cols], out_sem.at[c])

    def remote(src, dst, send, recv, k):
        return pltpu.make_async_remote_copy(
            src_ref=src, dst_ref=dst, send_sem=send, recv_sem=recv,
            device_id={"role": lax.rem(role + k, n)}, device_id_type=MESH,
        )

    def ids_remote(k):
        return remote(ids_ref, ids_in.at[k - 1], ids_send.at[k - 1], ids_recv.at[k - 1], k)

    def k_remote(k, c):
        return remote(side(0, c), k_in.at[k - 1, c], k_send.at[k - 1, c], k_recv.at[k - 1, c], k)

    def v_remote(k, c):
        return remote(side(1, c), v_in.at[k - 1, c], v_send.at[k - 1, c], v_recv.at[k - 1, c], k)

    for c in range(kvc):
        q_copy(c).start()
        k_copy(c).start()
        v_copy(c).start()
    if n > 1:
        pl.semaphore_wait(barrier, n - 1)
    for k in range(1, n):

        @pl.when(role + k < n)
        def _():
            ids_remote(k).start()
            for c in range(kvc):
                k_remote(k, c).start()
            for c in range(kvc):
                v_remote(k, c).start()

    ids_row = ids_ref[...]
    ids_col[...] = jnp.transpose(jnp.broadcast_to(ids_row, (HD, rows)))

    def wide(part, times):
        return jnp.concatenate([part] * times, axis=1) if times > 1 else part

    for t in range(tiles):
        r = slice(t * TILE, (t + 1) * TILE)
        w = (t + 1) * TILE
        row_at = lax.broadcasted_iota(jnp.int32, (TILE, w), 0) + t * TILE
        col_at = lax.broadcasted_iota(jnp.int32, (TILE, w), 1)
        same = wide(ids_col[r, :], w // HD) == ids_row[:, :w]
        bias[r, :w] = jnp.where(same & (col_at <= row_at), 0.0, HIDDEN)

    def head_cols(h):
        return pl.ds(pl.multiple_of(h * HD, HD), HD)

    def own(c, j):
        h = c * share + j
        for t in range(tiles):
            r = slice(t * TILE, (t + 1) * TILE)
            w = (t + 1) * TILE
            s = dot_t(q[r, head_cols(h)], k_own[c, :w, :]) + bias[r, :w]
            largest = jnp.max(s, axis=1, keepdims=True)
            e = jnp.exp2((s - largest) * rate)
            top[h, r, :] = jnp.broadcast_to(largest, (TILE, HD))
            total[h, r, :] = jnp.broadcast_to(jnp.sum(e, axis=1, keepdims=True), (TILE, HD))
            acc[h, r, :] = dot(e.astype(jnp.bfloat16), v_own[c, :w, :])

    for c in range(kvc):
        q_copy(c).wait()
        k_copy(c).wait()
        v_copy(c).wait()
        lax.fori_loop(0, share, lambda j, carry: (own(c, j), carry)[1], 0)

    def weigh(k, c, j):
        h = c * share + j
        for t in range(tiles):
            r = slice(t * TILE, (t + 1) * TILE)
            s = dot_t(q[r, head_cols(h)], k_in[k - 1, c]) + bias[r, :]
            before = top[h, r, :]
            largest = jnp.maximum(before, jnp.max(s, axis=1, keepdims=True))
            e = jnp.exp2((s - wide(largest, rows // HD)) * rate)
            factor = jnp.exp2((before - largest) * rate)
            weights[h, r, :] = e.astype(jnp.bfloat16)
            top[h, r, :] = largest
            total[h, r, :] = total[h, r, :] * factor + jnp.sum(e, axis=1, keepdims=True)
            acc[h, r, :] = acc[h, r, :] * factor

    def add_values(k, c, j):
        h = c * share + j
        acc[h] = acc[h] + dot(weights[h], v_in[k - 1, c])

    def finish_values(k, c, j):
        h = c * share + j
        summed = acc[h] + dot(weights[h], v_in[k - 1, c])
        out_buf[:, head_cols(h)] = (summed / total[h]).astype(jnp.bfloat16)

    def finish_own(c, j):
        h = c * share + j
        out_buf[:, head_cols(h)] = (acc[h] / total[h]).astype(jnp.bfloat16)

    def each(body):
        lax.fori_loop(0, share, lambda j, carry: (body(j), carry)[1], 0)

    for k in range(1, n):

        @pl.when(role >= k)
        def _():
            ids_remote(k).wait_recv()
            same = wide(ids_col[...], rows // HD) == ids_in[k - 1]
            bias[...] = jnp.where(same, 0.0, HIDDEN)
            for c in range(kvc):
                k_remote(k, c).wait_recv()
                each(functools.partial(weigh, k, c))
            for c in range(kvc):
                v_remote(k, c).wait_recv()

                @pl.when(role > k)
                def _():
                    each(functools.partial(add_values, k, c))

                @pl.when(role == k)
                def _():
                    each(functools.partial(finish_values, k, c))
                    out_copy(c).start()

    @pl.when(role == 0)
    def _():
        for c in range(kvc):
            each(functools.partial(finish_own, c))
            out_copy(c).start()

    for c in range(kvc):
        out_copy(c).wait()
    for k in range(1, n):

        @pl.when(role + k < n)
        def _():
            ids_remote(k).wait_send()
            for c in range(kvc):
                k_remote(k, c).wait_send()
                v_remote(k, c).wait_send()


def solution(mesh):
    n = mesh.shape["role"]
    parts = mesh.shape["tensor"]

    def per_device(queries, keys_values, doc_ids):
        rows, width_here = queries.shape
        heads = width_here // HD
        group_width = heads * parts // (keys_values.shape[2] // HD)
        kvc = max(1, heads // group_width)
        share = heads // kvc
        past = max(1, n - 1)
        bf16, f32, i32 = jnp.bfloat16, jnp.float32, jnp.int32
        dma = pltpu.SemaphoreType.DMA
        return pl.pallas_call(
            functools.partial(kernel, n, kvc, share, group_width),
            out_shape=jax.ShapeDtypeStruct((rows, width_here), bf16),
            in_specs=[
                pl.BlockSpec(memory_space=pl.ANY),
                pl.BlockSpec(memory_space=pl.ANY),
                pl.BlockSpec(memory_space=pltpu.VMEM),
            ],
            out_specs=pl.BlockSpec(memory_space=pl.ANY),
            scratch_shapes=[
                pltpu.VMEM((rows, width_here), bf16),
                pltpu.VMEM((kvc, rows, HD), bf16),
                pltpu.VMEM((kvc, rows, HD), bf16),
                pltpu.VMEM((past, kvc, rows, HD), bf16),
                pltpu.VMEM((past, kvc, rows, HD), bf16),
                pltpu.VMEM((past, 1, rows), i32),
                pltpu.VMEM((rows, HD), i32),
                pltpu.VMEM((rows, rows), f32),
                pltpu.VMEM((heads, rows, rows), bf16),
                pltpu.VMEM((heads, rows, HD), f32),
                pltpu.VMEM((heads, rows, HD), f32),
                pltpu.VMEM((heads, rows, HD), f32),
                pltpu.VMEM((rows, width_here), bf16),
                dma((kvc,)), dma((kvc,)), dma((kvc,)), dma((kvc,)),
                dma((past,)), dma((past,)),
                dma((past, kvc)), dma((past, kvc)), dma((past, kvc)), dma((past, kvc)),
            ],
            compiler_params=pltpu.CompilerParams(
                collective_id=0, has_side_effects=True, vmem_limit_bytes=40 << 20
            ),
        )(queries, keys_values, doc_ids[None])

    return jax.shard_map(
        per_device,
        mesh=mesh,
        in_specs=(
            P(("group", "role"), "tensor"),
            P(None, ("group", "role"), None),
            P(("group", "role")),
        ),
        out_specs=P(("group", "role"), "tensor"),
        check_vma=False,
    )
```

```python
import functools
import math

import jax
import jax.numpy as jnp
from jax import lax
from jax.experimental import pallas as pl
from jax.experimental.pallas import tpu as pltpu
from jax.sharding import PartitionSpec as P

HD = 128
TILE = 128
HIDDEN = -1e30
MESH = pl.DeviceIdType.MESH


def dot_t(a, b):
    return lax.dot_general(a, b, (((1,), (1,)), ((), ())), preferred_element_type=jnp.float32)


def dot(a, b):
    return lax.dot_general(a, b, (((1,), (0,)), ((), ())), preferred_element_type=jnp.float32)


def kernel(
    n, kvc, share, group_width, q_hbm, kv_hbm, ids_hbm, out_hbm,
    q, k_own, v_own, k_in, v_in, ids_own, ids_in, ids_col, bias, weights, acc, top, total, out_buf,
    ids_sem, q_sem, k_sem, v_sem, out_sem, ids_send, ids_recv, k_send, k_recv, v_send, v_recv,
):
    rows = q_hbm.shape[0]
    heads = kvc * share
    tiles = rows // TILE
    width = share * HD
    role = lax.axis_index("role")
    first_kv = lax.axis_index("tensor") * heads // group_width
    rate = math.log2(math.e) / math.sqrt(HD)

    barrier = pltpu.get_barrier_semaphore()
    for k in range(1, n):
        pl.semaphore_signal(
            barrier, inc=1, device_id={"role": lax.rem(role + k, n)}, device_id_type=MESH
        )

    def side(which, c):
        return kv_hbm.at[which, :, pl.ds(pl.multiple_of((first_kv + c) * HD, HD), HD)]

    def q_copy(c):
        cols = slice(c * width, (c + 1) * width)
        return pltpu.make_async_copy(q_hbm.at[:, cols], q.at[:, cols], q_sem.at[c])

    def k_copy(c):
        return pltpu.make_async_copy(side(0, c), k_own.at[c], k_sem.at[c])

    def v_copy(c):
        return pltpu.make_async_copy(side(1, c), v_own.at[c], v_sem.at[c])

    def out_copy(c):
        cols = slice(c * width, (c + 1) * width)
        return pltpu.make_async_copy(out_buf.at[:, cols], out_hbm.at[:, cols], out_sem.at[c])

    def remote(src, dst, send, recv, k):
        return pltpu.make_async_remote_copy(
            src_ref=src, dst_ref=dst, send_sem=send, recv_sem=recv,
            device_id={"role": lax.rem(role + k, n)}, device_id_type=MESH,
        )

    def ids_remote(k):
        return remote(ids_hbm, ids_in.at[k - 1], ids_send.at[k - 1], ids_recv.at[k - 1], k)

    def k_remote(k, c):
        return remote(side(0, c), k_in.at[k - 1, c], k_send.at[k - 1, c], k_recv.at[k - 1, c], k)

    def v_remote(k, c):
        return remote(side(1, c), v_in.at[k - 1, c], v_send.at[k - 1, c], v_recv.at[k - 1, c], k)

    ids_copy = pltpu.make_async_copy(ids_hbm, ids_own, ids_sem)
    ids_copy.start()
    for c in range(kvc):
        q_copy(c).start()
        k_copy(c).start()
        v_copy(c).start()
    if n > 1:
        pl.semaphore_wait(barrier, n - 1)
    for k in range(1, n):

        @pl.when(role + k < n)
        def _():
            ids_remote(k).start()
            for c in range(kvc):
                k_remote(k, c).start()
            for c in range(kvc):
                v_remote(k, c).start()

    ids_copy.wait()
    ids_row = ids_own[...]
    ids_col[...] = jnp.transpose(jnp.broadcast_to(ids_row, (HD, rows)))

    def wide(part, times):
        return jnp.concatenate([part] * times, axis=1) if times > 1 else part

    for t in range(tiles):
        r = slice(t * TILE, (t + 1) * TILE)
        w = (t + 1) * TILE
        row_at = lax.broadcasted_iota(jnp.int32, (TILE, w), 0) + t * TILE
        col_at = lax.broadcasted_iota(jnp.int32, (TILE, w), 1)
        same = wide(ids_col[r, :], w // HD) == ids_row[:, :w]
        bias[r, :w] = jnp.where(same & (col_at <= row_at), 0.0, HIDDEN)

    def head_cols(h):
        return pl.ds(pl.multiple_of(h * HD, HD), HD)

    def own(c, j):
        h = c * share + j
        for t in range(tiles):
            r = slice(t * TILE, (t + 1) * TILE)
            w = (t + 1) * TILE
            s = dot_t(q[r, head_cols(h)], k_own[c, :w, :]) + bias[r, :w]
            largest = jnp.max(s, axis=1, keepdims=True)
            e = jnp.exp2((s - largest) * rate)
            top[h, r, :] = jnp.broadcast_to(largest, (TILE, HD))
            total[h, r, :] = jnp.broadcast_to(jnp.sum(e, axis=1, keepdims=True), (TILE, HD))
            acc[h, r, :] = dot(e.astype(jnp.bfloat16), v_own[c, :w, :])

    for c in range(kvc):
        q_copy(c).wait()
        k_copy(c).wait()
        v_copy(c).wait()
        lax.fori_loop(0, share, lambda j, carry: (own(c, j), carry)[1], 0)

    def weigh(k, c, j):
        h = c * share + j
        for t in range(tiles):
            r = slice(t * TILE, (t + 1) * TILE)
            s = dot_t(q[r, head_cols(h)], k_in[k - 1, c]) + bias[r, :]
            before = top[h, r, :]
            largest = jnp.maximum(before, jnp.max(s, axis=1, keepdims=True))
            e = jnp.exp2((s - wide(largest, rows // HD)) * rate)
            factor = jnp.exp2((before - largest) * rate)
            weights[h, r, :] = e.astype(jnp.bfloat16)
            top[h, r, :] = largest
            total[h, r, :] = total[h, r, :] * factor + jnp.sum(e, axis=1, keepdims=True)
            acc[h, r, :] = acc[h, r, :] * factor

    def add_values(k, c, j):
        h = c * share + j
        acc[h] = acc[h] + dot(weights[h], v_in[k - 1, c])

    def finish_values(k, c, j):
        h = c * share + j
        summed = acc[h] + dot(weights[h], v_in[k - 1, c])
        out_buf[:, head_cols(h)] = (summed / total[h]).astype(jnp.bfloat16)

    def finish_own(c, j):
        h = c * share + j
        out_buf[:, head_cols(h)] = (acc[h] / total[h]).astype(jnp.bfloat16)

    def each(body):
        lax.fori_loop(0, share, lambda j, carry: (body(j), carry)[1], 0)

    for k in range(1, n):

        @pl.when(role >= k)
        def _():
            ids_remote(k).wait_recv()
            same = wide(ids_col[...], rows // HD) == ids_in[k - 1]
            bias[...] = jnp.where(same, 0.0, HIDDEN)
            for c in range(kvc):
                k_remote(k, c).wait_recv()
                each(functools.partial(weigh, k, c))
            for c in range(kvc):
                v_remote(k, c).wait_recv()

                @pl.when(role > k)
                def _():
                    each(functools.partial(add_values, k, c))

                @pl.when(role == k)
                def _():
                    each(functools.partial(finish_values, k, c))
                    out_copy(c).start()

    @pl.when(role == 0)
    def _():
        for c in range(kvc):
            each(functools.partial(finish_own, c))
            out_copy(c).start()

    for c in range(kvc):
        out_copy(c).wait()
    for k in range(1, n):

        @pl.when(role + k < n)
        def _():
            ids_remote(k).wait_send()
            for c in range(kvc):
                k_remote(k, c).wait_send()
                v_remote(k, c).wait_send()


def solution(mesh):
    n = mesh.shape["role"]
    parts = mesh.shape["tensor"]

    def per_device(queries, keys_values, doc_ids):
        rows, width_here = queries.shape
        heads = width_here // HD
        group_width = heads * parts // (keys_values.shape[2] // HD)
        kvc = max(1, heads // group_width)
        share = heads // kvc
        past = max(1, n - 1)
        bf16, f32, i32 = jnp.bfloat16, jnp.float32, jnp.int32
        dma = pltpu.SemaphoreType.DMA
        return pl.pallas_call(
            functools.partial(kernel, n, kvc, share, group_width),
            out_shape=jax.ShapeDtypeStruct((rows, width_here), bf16),
            in_specs=[
                pl.BlockSpec(memory_space=pl.ANY),
                pl.BlockSpec(memory_space=pl.ANY),
                pl.BlockSpec(memory_space=pl.ANY),
            ],
            out_specs=pl.BlockSpec(memory_space=pl.ANY),
            scratch_shapes=[
                pltpu.VMEM((rows, width_here), bf16),
                pltpu.VMEM((kvc, rows, HD), bf16),
                pltpu.VMEM((kvc, rows, HD), bf16),
                pltpu.VMEM((past, kvc, rows, HD), bf16),
                pltpu.VMEM((past, kvc, rows, HD), bf16),
                pltpu.VMEM((1, rows), i32),
                pltpu.VMEM((past, 1, rows), i32),
                pltpu.VMEM((rows, HD), i32),
                pltpu.VMEM((rows, rows), f32),
                pltpu.VMEM((heads, rows, rows), bf16),
                pltpu.VMEM((heads, rows, HD), f32),
                pltpu.VMEM((heads, rows, HD), f32),
                pltpu.VMEM((heads, rows, HD), f32),
                pltpu.VMEM((rows, width_here), bf16),
                dma, dma((kvc,)), dma((kvc,)), dma((kvc,)), dma((kvc,)),
                dma((past,)), dma((past,)),
                dma((past, kvc)), dma((past, kvc)), dma((past, kvc)), dma((past, kvc)),
            ],
            compiler_params=pltpu.CompilerParams(
                collective_id=0, has_side_effects=True, vmem_limit_bytes=40 << 20
            ),
        )(
            pltpu.with_memory_space_constraint(queries, pltpu.HBM),
            pltpu.with_memory_space_constraint(keys_values, pltpu.HBM),
            pltpu.with_memory_space_constraint(doc_ids[None], pltpu.HBM),
        )

    return jax.shard_map(
        per_device,
        mesh=mesh,
        in_specs=(
            P(("group", "role"), "tensor"),
            P(None, ("group", "role"), None),
            P(("group", "role")),
        ),
        out_specs=P(("group", "role"), "tensor"),
        check_vma=False,
    )
```

```python
import functools
import math

import jax
import jax.numpy as jnp
from jax import lax
from jax.experimental import pallas as pl
from jax.experimental.pallas import tpu as pltpu
from jax.sharding import PartitionSpec as P

HD = 128
OWN = 256
REM = 256
HIDDEN = -1e30
MESH = pl.DeviceIdType.MESH


def dot_t(a, b):
    return lax.dot_general(a, b, (((1,), (1,)), ((), ())), preferred_element_type=jnp.float32)


def dot(a, b):
    return lax.dot_general(a, b, (((1,), (0,)), ((), ())), preferred_element_type=jnp.float32)


def kernel(
    n, kvc, share, group_width, q_hbm, kv_hbm, ids_hbm, out,
    q, k_own, v_own, k_in, v_in, ids_own, ids_in, ids_col, bias, weights, acc, top, total,
    ids_sem, q_sem, k_sem, v_sem, ids_send, ids_recv, k_send, k_recv, v_send, v_recv,
):
    rows = q_hbm.shape[0]
    heads = kvc * share
    width = share * HD
    role = lax.axis_index("role")
    first_kv = lax.axis_index("tensor") * heads // group_width
    rate = math.log2(math.e) / math.sqrt(HD)

    barrier = pltpu.get_barrier_semaphore()
    for k in range(1, n):
        pl.semaphore_signal(
            barrier, inc=1, device_id={"role": lax.rem(role + k, n)}, device_id_type=MESH
        )

    def side(which, c):
        return kv_hbm.at[which, :, pl.ds(pl.multiple_of((first_kv + c) * HD, HD), HD)]

    def q_copy(c):
        cols = slice(c * width, (c + 1) * width)
        return pltpu.make_async_copy(q_hbm.at[:, cols], q.at[:, cols], q_sem.at[c])

    def k_copy(c):
        return pltpu.make_async_copy(side(0, c), k_own.at[c], k_sem.at[c])

    def v_copy(c):
        return pltpu.make_async_copy(side(1, c), v_own.at[c], v_sem.at[c])

    def remote(src, dst, send, recv, k):
        return pltpu.make_async_remote_copy(
            src_ref=src, dst_ref=dst, send_sem=send, recv_sem=recv,
            device_id={"role": lax.rem(role + k, n)}, device_id_type=MESH,
        )

    def ids_remote(k):
        return remote(ids_hbm, ids_in.at[k - 1], ids_send.at[k - 1], ids_recv.at[k - 1], k)

    def k_remote(k, c):
        return remote(side(0, c), k_in.at[k - 1, c], k_send.at[k - 1, c], k_recv.at[k - 1, c], k)

    def v_remote(k, c):
        return remote(side(1, c), v_in.at[k - 1, c], v_send.at[k - 1, c], v_recv.at[k - 1, c], k)

    ids_copy = pltpu.make_async_copy(ids_hbm, ids_own, ids_sem)
    ids_copy.start()
    for c in range(kvc):
        q_copy(c).start()
        k_copy(c).start()
        v_copy(c).start()
    if n > 1:
        pl.semaphore_wait(barrier, n - 1)
    for k in range(1, n):

        @pl.when(role + k < n)
        def _():
            ids_remote(k).start()
            for c in range(kvc):
                k_remote(k, c).start()
            for c in range(kvc):
                v_remote(k, c).start()

    ids_copy.wait()
    ids_row = ids_own[...]
    ids_col[...] = jnp.transpose(jnp.broadcast_to(ids_row, (HD, rows)))

    def wide(part, times):
        return jnp.concatenate([part] * times, axis=1) if times > 1 else part

    for t in range(rows // OWN):
        r = slice(t * OWN, (t + 1) * OWN)
        w = (t + 1) * OWN
        row_at = lax.broadcasted_iota(jnp.int32, (OWN, w), 0) + t * OWN
        col_at = lax.broadcasted_iota(jnp.int32, (OWN, w), 1)
        same = wide(ids_col[r, :], w // HD) == ids_row[:, :w]
        bias[r, :w] = jnp.where(same & (col_at <= row_at), 0.0, HIDDEN)

    def head_cols(h):
        return pl.ds(pl.multiple_of(h * HD, HD), HD)

    def own(c, j):
        h = c * share + j
        for t in range(rows // OWN):
            r = slice(t * OWN, (t + 1) * OWN)
            w = (t + 1) * OWN
            s = dot_t(q[r, head_cols(h)], k_own[c, :w, :]) + bias[r, :w]
            largest = jnp.max(s, axis=1, keepdims=True)
            e = jnp.exp2((s - largest) * rate)
            top[h, r, :] = jnp.broadcast_to(largest, (OWN, HD))
            total[h, r, :] = jnp.broadcast_to(jnp.sum(e, axis=1, keepdims=True), (OWN, HD))
            acc[h, r, :] = dot(e.astype(jnp.bfloat16), v_own[c, :w, :])

    for c in range(kvc):
        q_copy(c).wait()
        k_copy(c).wait()
        v_copy(c).wait()
        lax.fori_loop(0, share, lambda j, carry: (own(c, j), carry)[1], 0, unroll=True)

    def weigh(k, c, j):
        h = c * share + j
        for t in range(rows // REM):
            r = slice(t * REM, (t + 1) * REM)
            s = dot_t(q[r, head_cols(h)], k_in[k - 1, c]) + bias[r, :]
            before = top[h, r, :]
            largest = jnp.maximum(before, jnp.max(s, axis=1, keepdims=True))
            e = jnp.exp2((s - wide(largest, rows // HD)) * rate)
            factor = jnp.exp2((before - largest) * rate)
            weights[h, r, :] = e.astype(jnp.bfloat16)
            top[h, r, :] = largest
            total[h, r, :] = total[h, r, :] * factor + jnp.sum(e, axis=1, keepdims=True)
            acc[h, r, :] = acc[h, r, :] * factor

    def add_values(k, c, j):
        h = c * share + j
        acc[h] = acc[h] + dot(weights[h], v_in[k - 1, c])

    def finish_values(k, c, j):
        h = c * share + j
        summed = acc[h] + dot(weights[h], v_in[k - 1, c])
        out[:, head_cols(h)] = (summed / total[h]).astype(jnp.bfloat16)

    def finish_own(c, j):
        h = c * share + j
        out[:, head_cols(h)] = (acc[h] / total[h]).astype(jnp.bfloat16)

    def each(body):
        lax.fori_loop(0, share, lambda j, carry: (body(j), carry)[1], 0, unroll=True)

    for k in range(1, n):

        @pl.when(role >= k)
        def _():
            ids_remote(k).wait_recv()
            same = wide(ids_col[...], rows // HD) == ids_in[k - 1]
            bias[...] = jnp.where(same, 0.0, HIDDEN)
            for c in range(kvc):
                k_remote(k, c).wait_recv()
                each(functools.partial(weigh, k, c))
            for c in range(kvc):
                v_remote(k, c).wait_recv()

                @pl.when(role > k)
                def _():
                    each(functools.partial(add_values, k, c))

                @pl.when(role == k)
                def _():
                    each(functools.partial(finish_values, k, c))

    @pl.when(role == 0)
    def _():
        for c in range(kvc):
            each(functools.partial(finish_own, c))

    for k in range(1, n):

        @pl.when(role + k < n)
        def _():
            ids_remote(k).wait_send()
            for c in range(kvc):
                k_remote(k, c).wait_send()
                v_remote(k, c).wait_send()


def solution(mesh):
    n = mesh.shape["role"]
    parts = mesh.shape["tensor"]

    def per_device(queries, keys_values, doc_ids):
        rows, width_here = queries.shape
        heads = width_here // HD
        group_width = heads * parts // (keys_values.shape[2] // HD)
        kvc = max(1, heads // group_width)
        share = heads // kvc
        past = max(1, n - 1)
        bf16, f32, i32 = jnp.bfloat16, jnp.float32, jnp.int32
        dma = pltpu.SemaphoreType.DMA
        return pl.pallas_call(
            functools.partial(kernel, n, kvc, share, group_width),
            out_shape=jax.ShapeDtypeStruct((rows, width_here), bf16),
            in_specs=[
                pl.BlockSpec(memory_space=pl.ANY),
                pl.BlockSpec(memory_space=pl.ANY),
                pl.BlockSpec(memory_space=pl.ANY),
            ],
            out_specs=pl.BlockSpec(memory_space=pltpu.VMEM),
            scratch_shapes=[
                pltpu.VMEM((rows, width_here), bf16),
                pltpu.VMEM((kvc, rows, HD), bf16),
                pltpu.VMEM((kvc, rows, HD), bf16),
                pltpu.VMEM((past, kvc, rows, HD), bf16),
                pltpu.VMEM((past, kvc, rows, HD), bf16),
                pltpu.VMEM((1, rows), i32),
                pltpu.VMEM((past, 1, rows), i32),
                pltpu.VMEM((rows, HD), i32),
                pltpu.VMEM((rows, rows), f32),
                pltpu.VMEM((heads, rows, rows), bf16),
                pltpu.VMEM((heads, rows, HD), f32),
                pltpu.VMEM((heads, rows, HD), f32),
                pltpu.VMEM((heads, rows, HD), f32),
                dma, dma((kvc,)), dma((kvc,)), dma((kvc,)),
                dma((past,)), dma((past,)),
                dma((past, kvc)), dma((past, kvc)), dma((past, kvc)), dma((past, kvc)),
            ],
            compiler_params=pltpu.CompilerParams(
                collective_id=0, has_side_effects=True, vmem_limit_bytes=40 << 20
            ),
        )(
            pltpu.with_memory_space_constraint(queries, pltpu.HBM),
            pltpu.with_memory_space_constraint(keys_values, pltpu.HBM),
            pltpu.with_memory_space_constraint(doc_ids[None], pltpu.HBM),
        )

    return jax.shard_map(
        per_device,
        mesh=mesh,
        in_specs=(
            P(("group", "role"), "tensor"),
            P(None, ("group", "role"), None),
            P(("group", "role")),
        ),
        out_specs=P(("group", "role"), "tensor"),
        check_vma=False,
    )
```

```python
import functools
import math

import jax
import jax.numpy as jnp
from jax import lax
from jax.experimental import pallas as pl
from jax.experimental.pallas import tpu as pltpu
from jax.sharding import PartitionSpec as P

HD = 128
OWN = 256
REM = 256
HIDDEN = -1e30
MESH = pl.DeviceIdType.MESH


def dot_t(a, b):
    return lax.dot_general(a, b, (((1,), (1,)), ((), ())), preferred_element_type=jnp.float32)


def dot(a, b):
    return lax.dot_general(a, b, (((1,), (0,)), ((), ())), preferred_element_type=jnp.float32)


def kernel(
    n, kvc, share, group_width, q_hbm, kv_hbm, ids_hbm, out,
    q, k_own, v_own, k_in, v_in, ids_own, ids_in, ids_col, bias, weights, acc, top, total,
    ids_sem, q_sem, k_sem, v_sem, ids_send, ids_recv, k_send, k_recv, v_send, v_recv,
):
    rows = q_hbm.shape[0]
    heads = kvc * share
    width = share * HD
    role = lax.axis_index("role")
    first_kv = lax.axis_index("tensor") * heads // group_width
    rate = math.log2(math.e) / math.sqrt(HD)

    barrier = pltpu.get_barrier_semaphore()
    for k in range(1, n):
        pl.semaphore_signal(
            barrier, inc=1, device_id={"role": lax.rem(role + k, n)}, device_id_type=MESH
        )

    def side(which, c):
        return kv_hbm.at[which, :, pl.ds(pl.multiple_of((first_kv + c) * HD, HD), HD)]

    def q_copy(c):
        cols = slice(c * width, (c + 1) * width)
        return pltpu.make_async_copy(q_hbm.at[:, cols], q.at[:, cols], q_sem.at[c])

    def k_copy(c):
        return pltpu.make_async_copy(side(0, c), k_own.at[c], k_sem.at[c])

    def v_copy(c):
        return pltpu.make_async_copy(side(1, c), v_own.at[c], v_sem.at[c])

    def remote(src, dst, send, recv, k):
        return pltpu.make_async_remote_copy(
            src_ref=src, dst_ref=dst, send_sem=send, recv_sem=recv,
            device_id={"role": lax.rem(role + k, n)}, device_id_type=MESH,
        )

    def ids_remote(k):
        return remote(ids_hbm, ids_in.at[k - 1], ids_send.at[k - 1], ids_recv.at[k - 1], k)

    def k_remote(k, c):
        return remote(side(0, c), k_in.at[k - 1, c], k_send.at[k - 1, c], k_recv.at[k - 1, c], k)

    half = rows // 2

    def v_remote(k, c, i):
        part = pl.ds(i * half, half)
        cols = pl.ds(pl.multiple_of((first_kv + c) * HD, HD), HD)
        at = 2 * c + i
        return remote(
            kv_hbm.at[1, part, cols], v_in.at[k - 1, c, part],
            v_send.at[k - 1, at], v_recv.at[k - 1, at], k,
        )

    ids_copy = pltpu.make_async_copy(ids_hbm, ids_own, ids_sem)
    ids_copy.start()
    for c in range(kvc):
        q_copy(c).start()
        k_copy(c).start()
        v_copy(c).start()
    if n > 1:
        pl.semaphore_wait(barrier, n - 1)
    for k in range(1, n):

        @pl.when(role + k < n)
        def _():
            ids_remote(k).start()
            for c in range(kvc):
                k_remote(k, c).start()
            for c in range(kvc):
                for i in range(2):
                    v_remote(k, c, i).start()

    ids_copy.wait()
    ids_row = ids_own[...]
    ids_col[...] = jnp.transpose(jnp.broadcast_to(ids_row, (HD, rows)))

    def wide(part, times):
        return jnp.concatenate([part] * times, axis=1) if times > 1 else part

    for t in range(rows // OWN):
        r = slice(t * OWN, (t + 1) * OWN)
        w = (t + 1) * OWN
        row_at = lax.broadcasted_iota(jnp.int32, (OWN, w), 0) + t * OWN
        col_at = lax.broadcasted_iota(jnp.int32, (OWN, w), 1)
        same = wide(ids_col[r, :], w // HD) == ids_row[:, :w]
        bias[r, :w] = jnp.where(same & (col_at <= row_at), 0.0, HIDDEN)

    def head_cols(h):
        return pl.ds(pl.multiple_of(h * HD, HD), HD)

    def own(c, j):
        h = c * share + j
        for t in range(rows // OWN):
            r = slice(t * OWN, (t + 1) * OWN)
            w = (t + 1) * OWN
            s = dot_t(q[r, head_cols(h)], k_own[c, :w, :]) + bias[r, :w]
            largest = jnp.max(s, axis=1, keepdims=True)
            e = jnp.exp2((s - largest) * rate)
            top[h, r, :] = jnp.broadcast_to(largest, (OWN, HD))
            total[h, r, :] = jnp.broadcast_to(jnp.sum(e, axis=1, keepdims=True), (OWN, HD))
            acc[h, r, :] = dot(e.astype(jnp.bfloat16), v_own[c, :w, :])

    for c in range(kvc):
        q_copy(c).wait()
        k_copy(c).wait()
        v_copy(c).wait()
        lax.fori_loop(0, share, lambda j, carry: (own(c, j), carry)[1], 0, unroll=True)

    def weigh(k, c, j):
        h = c * share + j
        for t in range(rows // REM):
            r = slice(t * REM, (t + 1) * REM)
            s = dot_t(q[r, head_cols(h)], k_in[k - 1, c]) + bias[r, :]
            before = top[h, r, :]
            largest = jnp.maximum(before, jnp.max(s, axis=1, keepdims=True))
            e = jnp.exp2((s - wide(largest, rows // HD)) * rate)
            factor = jnp.exp2((before - largest) * rate)
            weights[h, r, :] = e.astype(jnp.bfloat16)
            top[h, r, :] = largest
            total[h, r, :] = total[h, r, :] * factor + jnp.sum(e, axis=1, keepdims=True)
            acc[h, r, :] = acc[h, r, :] * factor

    def add_values(k, c, j):
        h = c * share + j
        acc[h] = acc[h] + dot(weights[h, :, :half], v_in[k - 1, c, :half])

    def add_rest(k, c, j):
        h = c * share + j
        acc[h] = acc[h] + dot(weights[h, :, half:], v_in[k - 1, c, half:])

    def finish_values(k, c, j):
        h = c * share + j
        summed = acc[h] + dot(weights[h, :, half:], v_in[k - 1, c, half:])
        out[:, head_cols(h)] = (summed / total[h]).astype(jnp.bfloat16)

    def finish_own(c, j):
        h = c * share + j
        out[:, head_cols(h)] = (acc[h] / total[h]).astype(jnp.bfloat16)

    def each(body):
        lax.fori_loop(0, share, lambda j, carry: (body(j), carry)[1], 0, unroll=True)

    for k in range(1, n):

        @pl.when(role >= k)
        def _():
            ids_remote(k).wait_recv()
            same = wide(ids_col[...], rows // HD) == ids_in[k - 1]
            bias[...] = jnp.where(same, 0.0, HIDDEN)
            for c in range(kvc):
                k_remote(k, c).wait_recv()
                each(functools.partial(weigh, k, c))
            for c in range(kvc):
                v_remote(k, c, 0).wait_recv()
                each(functools.partial(add_values, k, c))
                v_remote(k, c, 1).wait_recv()

                @pl.when(role > k)
                def _():
                    each(functools.partial(add_rest, k, c))

                @pl.when(role == k)
                def _():
                    each(functools.partial(finish_values, k, c))

    @pl.when(role == 0)
    def _():
        for c in range(kvc):
            each(functools.partial(finish_own, c))

    for k in range(1, n):

        @pl.when(role + k < n)
        def _():
            ids_remote(k).wait_send()
            for c in range(kvc):
                k_remote(k, c).wait_send()
                for i in range(2):
                    v_remote(k, c, i).wait_send()


def solution(mesh):
    n = mesh.shape["role"]
    parts = mesh.shape["tensor"]

    def per_device(queries, keys_values, doc_ids):
        rows, width_here = queries.shape
        heads = width_here // HD
        group_width = heads * parts // (keys_values.shape[2] // HD)
        kvc = max(1, heads // group_width)
        share = heads // kvc
        past = max(1, n - 1)
        bf16, f32, i32 = jnp.bfloat16, jnp.float32, jnp.int32
        dma = pltpu.SemaphoreType.DMA
        return pl.pallas_call(
            functools.partial(kernel, n, kvc, share, group_width),
            out_shape=jax.ShapeDtypeStruct((rows, width_here), bf16),
            in_specs=[
                pl.BlockSpec(memory_space=pl.ANY),
                pl.BlockSpec(memory_space=pl.ANY),
                pl.BlockSpec(memory_space=pl.ANY),
            ],
            out_specs=pl.BlockSpec(memory_space=pltpu.VMEM),
            scratch_shapes=[
                pltpu.VMEM((rows, width_here), bf16),
                pltpu.VMEM((kvc, rows, HD), bf16),
                pltpu.VMEM((kvc, rows, HD), bf16),
                pltpu.VMEM((past, kvc, rows, HD), bf16),
                pltpu.VMEM((past, kvc, rows, HD), bf16),
                pltpu.VMEM((1, rows), i32),
                pltpu.VMEM((past, 1, rows), i32),
                pltpu.VMEM((rows, HD), i32),
                pltpu.VMEM((rows, rows), f32),
                pltpu.VMEM((heads, rows, rows), bf16),
                pltpu.VMEM((heads, rows, HD), f32),
                pltpu.VMEM((heads, rows, HD), f32),
                pltpu.VMEM((heads, rows, HD), f32),
                dma, dma((kvc,)), dma((kvc,)), dma((kvc,)),
                dma((past,)), dma((past,)),
                dma((past, kvc)), dma((past, kvc)), dma((past, 2 * kvc)), dma((past, 2 * kvc)),
            ],
            compiler_params=pltpu.CompilerParams(
                collective_id=0, has_side_effects=True, vmem_limit_bytes=40 << 20
            ),
        )(
            pltpu.with_memory_space_constraint(queries, pltpu.HBM),
            pltpu.with_memory_space_constraint(keys_values, pltpu.HBM),
            pltpu.with_memory_space_constraint(doc_ids[None], pltpu.HBM),
        )

    return jax.shard_map(
        per_device,
        mesh=mesh,
        in_specs=(
            P(("group", "role"), "tensor"),
            P(None, ("group", "role"), None),
            P(("group", "role")),
        ),
        out_specs=P(("group", "role"), "tensor"),
        check_vma=False,
    )
```
